32 devices in a mesh: grp: 2 (over x), tm: 16 (over z, y, core).
Axes of the slice: x: 2, y: 2, z: 4, core: 2. Of those that a mesh axis runs over, the one named last changes fastest.
Arguments:
- dyn_a: float32 [128, 4, 64, 64], P('tm', 'grp'), parts along dimension 1, may hold values from -1 to 1
- dyn_b: float32 [128, 4, 64, 32], P('tm', 'grp'), parts along dimension 1, may hold values from -0.109375 to 0.109375
- gains: float32 [128, 4, 32, 64], P('tm', 'grp'), parts along dimension 1, may hold values from -0.2 to 0.2
- defects: float32 [128, 4, 64], P('tm', 'grp'), parts along dimension 1, may hold values from -6 to 6
- state_grad: float32 [128, 4, 64], P('tm', 'grp'), parts along dimension 1, may hold values from -6 to 6
- control_grad: float32 [128, 4, 32], P('tm', 'grp'), parts along dimension 1, may hold values from -1.5 to 1.5
- cost_factor: float32 [64, 64], replicated, may hold values from -0.75 to 0.75
- control_factor: float32 [32, 32], replicated, may hold values from -1 to 1
- init_state: float32 [4, 64], P('grp'), parts along dimension 0, may hold values from -6 to 6
Outputs:
- new_gains: float32 [128, 4, 32, 64], P('tm', 'grp'), parts along dimension 1
- feedforward: float32 [128, 4, 32], P('tm', 'grp'), parts along dimension 1
- states: float32 [128, 4, 64], P('tm', 'grp'), parts along dimension 1
- controls: float32 [128, 4, 32], P('tm', 'grp'), parts along dimension 1
- decrease: float32 [4], P('grp'), parts along dimension 0
The draws below stay inside these ranges and needn't reach their ends.
There are 2 independent parts, one for each index of `grp`. The reference program is written for one: setup_inputs(seed, part) draws one part's arguments, and reference() takes and returns one part's arrays. A program takes and returns all parts, laid end to end along the dimension named above; an argument that names none is the same for every part. Nothing has to cross between parts.
All inputs are finite; a program needn't handle non-finite values.
Results may differ from the reference program's by a relative error of at most 0.0003.
Values sent between devices are 32-bit elements; how exact they have to be, the bound alone decides.
A program may use at most 64 MiB of HBM per device.

```python
import math
import jax
import jax.numpy as jnp
from jax import lax

STATE_DIM = 64
NU = 32
TRAJECTORY_COUNT = 2
HORIZON_KNOTS = 128


def draw_dyn_a(key, part):
    random_keys = jax.random.split(jax.random.fold_in(key, 11), 7)
    share = 0.5
    sluggish_knots = jax.random.uniform(random_keys[0], (TRAJECTORY_COUNT, STATE_DIM)) < share
    fast_len = jax.random.uniform(random_keys[1], (TRAJECTORY_COUNT, STATE_DIM), minval=30.0, maxval=50.0)
    slow_len = 4.0 * HORIZON_KNOTS * jax.random.uniform(random_keys[2], (TRAJECTORY_COUNT, STATE_DIM), minval=1.0, maxval=3.0)
    length = jnp.where(sluggish_knots, slow_len, fast_len)
    jitter = jax.random.uniform(random_keys[3], (HORIZON_KNOTS, TRAJECTORY_COUNT, STATE_DIM), minval=0.5, maxval=1.5)
    decay_rate = jnp.exp(-jitter / length[None])
    spike_positions = jax.random.randint(random_keys[4], (3,), 0, HORIZON_KNOTS)
    knot_index = jnp.arange(HORIZON_KNOTS)
    spike_knots = jnp.any(knot_index[:, None] == spike_positions[None, :], axis=1)
    spike_multiplier = jax.random.uniform(random_keys[5], (HORIZON_KNOTS, TRAJECTORY_COUNT, STATE_DIM), minval=0.6, maxval=0.85)
    decay_rate = jnp.where(spike_knots[:, None, None] & sluggish_knots[None], decay_rate * spike_multiplier, decay_rate)
    raw = jax.random.normal(random_keys[6], (HORIZON_KNOTS, TRAJECTORY_COUNT, STATE_DIM, STATE_DIM), jnp.float32) * (0.6 / STATE_DIM ** 0.5)
    skew = 0.5 * (raw - jnp.swapaxes(raw, -1, -2))
    same = (sluggish_knots[:, :, None] == sluggish_knots[:, None, :]).astype(jnp.float32)
    skew = skew * same[None]
    eye = jnp.eye(STATE_DIM, dtype=jnp.float32)
    rotation = jnp.linalg.solve(eye + skew, jnp.broadcast_to(eye, skew.shape) - skew)
    return decay_rate[..., :, None] * rotation


def level_of(stream_key, shape, pieces, least, largest):
    factor_of, own = 1.0, jax.random.fold_in(stream_key, 6)
    for axis_at, blocks in pieces:
        draws = jnp.exp(jax.random.uniform(jax.random.fold_in(own, axis_at), (blocks,), jnp.float32, least / len(pieces), largest / len(pieces)))
        factor_of = factor_of * jnp.repeat(draws, shape[axis_at] // blocks).reshape([-1 if axis == axis_at else 1 for axis in range(len(shape))])
    return factor_of


def scatter_about(key, shape, deviation, reach, cuts=(), kind=jnp.bfloat16):
    result = deviation * jax.random.normal(key, shape, jnp.float32)
    if cuts:
        result = result * level_of(key, shape, cuts, -0.22, 0.18)
    return jnp.clip(result, -reach, reach).astype(kind)


def setup_inputs(seed: int = 0, part: int = 0) -> dict:
    seeds = jax.random.split(jax.random.key(seed), 10)
    part_keys = jax.random.split(jax.random.fold_in(seeds[9], part), 10)
    return {
        "dyn_a": draw_dyn_a(jax.random.fold_in(jax.random.fold_in(seeds[9], part), 71), part),
        "dyn_b": scatter_about(part_keys[1], (HORIZON_KNOTS, TRAJECTORY_COUNT, STATE_DIM, NU), (48 * STATE_DIM) ** -0.5, 0.109375, ((0, 16),), jnp.float32),
        "gains": scatter_about(part_keys[2], (HORIZON_KNOTS, TRAJECTORY_COUNT, NU, STATE_DIM), 0.03, 0.2, ((0, 16),), jnp.float32),
        "defects": scatter_about(part_keys[3], (HORIZON_KNOTS, TRAJECTORY_COUNT, STATE_DIM), 1.0, 6.0, ((0, 16),), jnp.float32),
        "state_grad": scatter_about(part_keys[4], (HORIZON_KNOTS, TRAJECTORY_COUNT, STATE_DIM), 1.0, 6.0, ((0, 16),), jnp.float32),
        "control_grad": scatter_about(part_keys[5], (HORIZON_KNOTS, TRAJECTORY_COUNT, NU), 0.25, 1.5, ((0, 16),), jnp.float32),
        "cost_factor": scatter_about(seeds[6], (STATE_DIM, STATE_DIM), STATE_DIM ** -0.5, 0.75, (), jnp.float32),
        "control_factor": scatter_about(seeds[7], (NU, NU), NU ** -0.5, 1.0, (), jnp.float32),
        "init_state": scatter_about(part_keys[8], (TRAJECTORY_COUNT, STATE_DIM), 1.0, 6.0, (), jnp.float32),
    }


def product(left, right):
    return jnp.matmul(left, right, precision=lax.Precision.HIGHEST)

def flipped(matrix):
    return jnp.swapaxes(matrix, -1, -2)

def apply_vec(matrix, vector):
    return product(matrix, vector[..., None])[..., 0]

def spd_solve(matrix, right_side):
    factor = jnp.linalg.cholesky(matrix)
    inner = jax.scipy.linalg.solve_triangular(factor, right_side, lower=True)
    return jax.scipy.linalg.solve_triangular(factor, inner, lower=True, trans=1)

def reference(dyn_a, dyn_b, gains, defects, state_grad, control_grad, cost_factor, control_factor, init_state):
    knots, trajs, width, controls_n = dyn_b.shape
    scale = 1.0 / math.sqrt(knots)
    term_q = jnp.eye(width, dtype=jnp.float32) + product(cost_factor, flipped(cost_factor))
    run_q = term_q / knots
    run_r = jnp.eye(controls_n, dtype=jnp.float32) + product(control_factor, flipped(control_factor))
    drift = defects * scale
    grad_q = state_grad * scale
    closed = dyn_a + product(dyn_b, gains)
    section_q = run_q + product(flipped(gains), product(run_r, gains))
    section_g = grad_q + apply_vec(flipped(gains), control_grad)

    def back_step(carry, item):
        value_mat, value_vec = carry
        a_mat, b_mat, f_mat, q_mat, d_vec, g_vec, r_vec = item
        value_b = product(value_mat, b_mat)
        hess = run_r + product(flipped(b_mat), value_b)
        cross = product(flipped(value_b), a_mat)
        lin = r_vec + apply_vec(flipped(b_mat), apply_vec(value_mat, d_vec) + value_vec)
        solved = spd_solve(hess, jnp.concatenate([cross, lin[..., None]], -1))
        new_gain = -solved[..., :width]
        feed = -solved[..., width]
        change = lax.optimization_barrier(jnp.sum(feed * lin, -1)) + 0.5 * lax.optimization_barrier(jnp.sum(feed * apply_vec(hess, feed), -1))
        next_mat = product(flipped(f_mat), product(value_mat, f_mat)) + q_mat
        next_vec = apply_vec(flipped(f_mat), value_vec + apply_vec(value_mat, d_vec)) + g_vec
        return ((next_mat, next_vec), (new_gain, feed, change))
    start = (jnp.broadcast_to(term_q, (trajs, width, width)), jnp.zeros((trajs, width), jnp.float32))
    items = (dyn_a, dyn_b, closed, section_q, drift, section_g, control_grad)
    _, (new_gains, feedforward, changes) = lax.scan(back_step, start, items, reverse=True)
    decrease = lax.optimization_barrier(jnp.sum(changes, 0)) / knots

    def forward_step(state, item):
        a_mat, b_mat, new_gain, feed, d_vec = item
        control = apply_vec(new_gain, state) + feed
        following = apply_vec(a_mat, state) + apply_vec(b_mat, control) + d_vec
        return (following, (state, control))
    _, (states, controls) = lax.scan(forward_step, init_state, (dyn_a, dyn_b, new_gains, feedforward, drift))
    return (new_gains, feedforward, states, controls, decrease)
```

```python
import functools
import math

import jax
import jax.numpy as jnp
from jax import lax
from jax.experimental import pallas as pl
from jax.experimental.pallas import tpu as pltpu
from jax.sharding import PartitionSpec as P

F32 = jnp.float32
BF16 = jnp.bfloat16
PAD = 8
MESH = pl.DeviceIdType.MESH
NN = (((1,), (0,)), ((), ()))
NT = (((1,), (1,)), ((), ()))


def split(a):
    hi = a.astype(BF16)
    return hi, (a - hi.astype(F32)).astype(BF16)


def dot3(a, b, dims=NN):
    ah, al = split(a)
    bh, bl = split(b)
    one = functools.partial(lax.dot_general, dimension_numbers=dims, preferred_element_type=F32)
    return one(ah, bh) + (one(ah, bl) + one(al, bh))


def with_row(matrix, row):
    first = lax.broadcasted_iota(jnp.int32, (PAD, row.shape[1]), 0) == 0
    return jnp.concatenate([matrix, jnp.where(first, row, 0.0)], 0)


def add_tail(a, tail):
    return jnp.concatenate([a[:-PAD], a[-PAD:] + tail], 0)


def compose_value(low, high):
    w = low.shape[1] // 2
    t = add_tail(dot3(low[:, :w], high[:w]), high[w:])
    right = dot3(t[:, w:], low[:w, :w], NT) + low[:, w:]
    return jnp.concatenate([t[:, :w], right], 1)


def apply_value(elem, value):
    w = value.shape[1]
    t = add_tail(dot3(elem[:, :w], value[:w]), value[w:])
    return dot3(t, elem[:w, :w], NT) + elem[:, w:]


def compose_state(low, high):
    w = low.shape[1]
    return add_tail(dot3(low, high[:w]), high[w:])


def place(tm):
    me = lax.axis_index("tm")
    rounds = tm.bit_length() - 1
    bits = [lax.rem(me // (1 << k), 2) for k in range(rounds)]
    partners = [me + (1 << k) * (1 - 2 * bits[k]) for k in range(rounds)]
    return bits, partners


def greet(partners):
    barrier = pltpu.get_barrier_semaphore()
    for partner in partners:
        pl.semaphore_signal(barrier, inc=1, device_id={"tm": partner}, device_id_type=MESH)


def greeted(partners):
    pl.semaphore_wait(pltpu.get_barrier_semaphore(), len(partners))


def exchange(src, dst, sems, k, partner):
    copy = pltpu.make_async_remote_copy(
        src_ref=src,
        dst_ref=dst,
        send_sem=sems.at[0, k],
        recv_sem=sems.at[1, k],
        device_id={"tm": partner},
        device_id_type=MESH,
    )
    copy.start()
    copy.wait()


def value_kernel(
    tm, a_ref, b_ref, k_ref, d_ref, sg_ref, cg_ref, cf_ref, rf_ref,
    elem_ref, end_ref, seg_ref, send_ref, recv_ref, psend_ref, precv_ref, sems,
):
    local, trajs, w, nu = b_ref.shape
    knots = local * tm
    scale = 1.0 / math.sqrt(knots)
    bits, partners = place(tm)
    greet(partners)
    eye = lambda n: (
        lax.broadcasted_iota(jnp.int32, (n, n), 0) == lax.broadcasted_iota(jnp.int32, (n, n), 1)
    ).astype(F32)
    term_q = eye(w) + dot3(cf_ref[...], cf_ref[...], NT)
    run_q = term_q / knots
    run_r = eye(nu) + dot3(rf_ref[...], rf_ref[...], NT)
    for t in range(local):
        for j in range(trajs):
            gain = k_ref[t, j]
            gain_t = gain.T
            g_mat = a_ref[t, j].T + dot3(gain_t, b_ref[t, j], NT)
            left = with_row(dot3(gain_t, run_r), cg_ref[t, j : j + 1])
            right = dot3(left, gain) + with_row(run_q, sg_ref[t, j : j + 1] * scale)
            elem_ref[t, j] = jnp.concatenate(
                [with_row(g_mat, d_ref[t, j : j + 1] * scale), right], 1
            )
    prev, base, count, at = elem_ref, 0, local, 0
    while count > 1:
        for i in range(count // 2):
            for j in range(trajs):
                seg_ref[at + i, j] = compose_value(prev[base + 2 * i, j], prev[base + 2 * i + 1, j])
        prev, base, at, count = seg_ref, at, at + count // 2, count // 2
    greeted(partners)
    totals = [prev[base, j] for j in range(trajs)]
    ident = with_row(
        jnp.concatenate([eye(w), jnp.zeros((w, w), F32)], 1), jnp.zeros((1, 2 * w), F32)
    )
    suffix = [ident] * trajs
    start = with_row(term_q, jnp.zeros((1, w), F32))
    last = len(partners) - 1
    for k in range(last):
        for j in range(trajs):
            send_ref[k, j] = totals[j]
        exchange(send_ref.at[k], recv_ref.at[k], sems, k, partners[k])
        up = bits[k] == 0
        for j in range(trajs):
            other = recv_ref[k, j]
            low = jnp.where(up, totals[j], other)
            high = jnp.where(up, other, totals[j])
            suffix[j] = jnp.where(up, compose_value(suffix[j], other), suffix[j])
            totals[j] = compose_value(low, high)
    if last >= 0:
        psend_ref[...] = jnp.concatenate([apply_value(totals[j], start) for j in range(trajs)], 1)
        exchange(psend_ref, precv_ref, sems, last, partners[last])
        up = bits[last] == 0
        for j in range(trajs):
            came = jnp.where(up, precv_ref[:, j * w : (j + 1) * w], start)
            end_ref[j] = apply_value(suffix[j], came)
    else:
        for j in range(trajs):
            end_ref[j] = start


def gain_kernel(
    knots, a_ref, b_ref, d_ref, cg_ref, rf_ref, elem_ref, seg_ref, end_ref,
    gain_ref, xt_ref, map_ref, fold_ref, tot_ref, val_ref, aug_ref,
):
    local, trajs, w, nu = b_ref.shape
    scale = 1.0 / math.sqrt(knots)
    eye = (
        lax.broadcasted_iota(jnp.int32, (nu, nu), 0) == lax.broadcasted_iota(jnp.int32, (nu, nu), 1)
    ).astype(F32)
    run_r = eye + dot3(rf_ref[...], rf_ref[...], NT)
    starts, count, at = [], local // 2, 0
    while count >= 1:
        starts.append(at)
        at += count
        count //= 2
    for j in range(trajs):
        val_ref[local - 1, j] = end_ref[j]
    half = local // 2
    while half >= 1:
        level = half.bit_length() - 1
        for i in range(local // (2 * half)):
            for j in range(trajs):
                hi = 2 * i + 1
                elem = elem_ref[hi, j] if level == 0 else seg_ref[starts[level - 1] + hi, j]
                val_ref[hi * half - 1, j] = apply_value(elem, val_ref[(hi + 1) * half - 1, j])
        half //= 2
    lane = lax.broadcasted_iota(jnp.int32, (nu, w + nu + PAD), 1)
    for t in range(local):
        cg_t = cg_ref[t].T
        for j in range(trajs):
            b_t = b_ref[t, j].T
            value = val_ref[t, j]
            rows = with_row(jnp.concatenate([a_ref[t, j].T, b_t], 0), d_ref[t, j : j + 1] * scale)
            y = add_tail(dot3(rows, value[:w]), value[w:])
            aug = dot3(b_t, y, NT)
            aug = aug + jnp.concatenate(
                [jnp.zeros((nu, w), F32), run_r, jnp.zeros((nu, PAD), F32)], 1
            )
            aug = jnp.where(lane == w + nu, aug + cg_t[:, j : j + 1], aug)
            aug_ref[t * trajs + j] = aug
    pairs = local * trajs
    group = min(8, pairs)
    sub = lax.broadcasted_iota(jnp.int32, (1, 8, 1), 1)
    for g0 in range(0, pairs, group):
        parts = [aug_ref[g0 : g0 + group, 8 * q : 8 * q + 8] for q in range(nu // 8)]
        for s in range(nu):
            q0, r0 = divmod(s, 8)
            pivot = parts[q0][:, r0 : r0 + 1]
            row = pivot / pivot[:, :, w + s : w + s + 1]
            for q in range(nu // 8):
                new = parts[q] - parts[q][:, :, w + s : w + s + 1] * row
                parts[q] = jnp.where(sub == r0, row, new) if q == q0 else new
        for g in range(group):
            t, j = divmod(g0 + g, trajs)
            x = jnp.concatenate([part[g] for part in parts], 0)
            gain_ref[t, j] = -x[:, :w]
            x_t = x.T
            xt = -jnp.concatenate([x_t[:w], x_t[w + nu :]], 0)
            xt_ref[t, j] = xt
            map_ref[t, j] = (
                dot3(xt, b_ref[t, j], NT) + with_row(a_ref[t, j].T, d_ref[t, j : j + 1] * scale)
            )
    prev, base, count, at = map_ref, 0, local, 0
    while count > 1:
        for i in range(count // 2):
            for j in range(trajs):
                fold_ref[at + i, j] = compose_state(
                    prev[base + 2 * i, j], prev[base + 2 * i + 1, j]
                )
        prev, base, at, count = fold_ref, at, at + count // 2, count // 2
    for j in range(trajs):
        tot_ref[0 : w + PAD, j * w : (j + 1) * w] = prev[base, j]
        total = jnp.zeros((nu, 1), F32)
        for t in range(local):
            aug = aug_ref[t * trajs + j]
            feed = xt_ref[t, j][w : w + 1]
            hess_feed = jnp.sum(aug[:, w : w + nu] * feed, 1, keepdims=True)
            back = dot3(eye, xt_ref[t, j][w:], NT)[:, :1]
            total = total + back * (aug[:, w + nu : w + nu + 1] + 0.5 * hess_feed)
        tot_ref[w + PAD :, j * w : (j + 1) * w] = jnp.broadcast_to(
            jnp.sum(total, 0, keepdims=True), (8, w)
        )


def state_kernel(
    tm, init_ref, xt_ref, map_ref, fold_ref, tot_ref,
    state_ref, control_ref, feed_ref, dec_ref, send_ref, recv_ref, sems,
):
    local, trajs, high, nu = xt_ref.shape
    w = high - PAD
    bits, partners = place(tm)
    greet(partners)
    for t in range(local):
        for j in range(trajs):
            feed_ref[t, j : j + 1] = xt_ref[t, j, w : w + 1]
    row0 = lax.broadcasted_iota(jnp.int32, (PAD, w), 0) == 0
    totals = [tot_ref[:high, j * w : (j + 1) * w] for j in range(trajs)]
    dec = tot_ref[high:]
    prefix = [jnp.where(row0, init_ref[j : j + 1], 0.0) for j in range(trajs)]
    ident = with_row(
        (
            lax.broadcasted_iota(jnp.int32, (w, w), 0) == lax.broadcasted_iota(jnp.int32, (w, w), 1)
        ).astype(F32),
        jnp.zeros((1, w), F32),
    )
    before = [ident] * trajs
    greeted(partners)
    for k in range(len(partners)):
        src = tot_ref
        if k > 0:
            for j in range(trajs):
                send_ref[k, :high, j * w : (j + 1) * w] = totals[j]
            send_ref[k, high:] = dec
            src = send_ref.at[k]
        exchange(src, recv_ref.at[k], sems, k, partners[k])
        dec = dec + recv_ref[k, high:]
        up = bits[k] == 0
        for j in range(trajs):
            other = recv_ref[k, :high, j * w : (j + 1) * w]
            before[j] = jnp.where(up, before[j], compose_state(other, before[j]))
            if k + 1 < len(partners):
                low = jnp.where(up, totals[j], other)
                top = jnp.where(up, other, totals[j])
                totals[j] = compose_state(low, top)
    starts, count, at = [], local // 2, 0
    while count >= 1:
        starts.append(at)
        at += count
        count //= 2
    for j in range(trajs):
        x = {0: dot3(prefix[j], before[j][:w]) + before[j][w:]}
        half = local // 2
        while half >= 1:
            level = half.bit_length() - 1
            for i in range(local // (2 * half)):
                elem = map_ref[2 * i, j] if level == 0 else fold_ref[starts[level - 1] + 2 * i, j]
                at_t = 2 * i * half
                x[at_t + half] = dot3(x[at_t], elem[:w]) + elem[w:]
            half //= 2
        for t in range(local):
            xt = xt_ref[t, j]
            state_ref[t, j : j + 1] = x[t][:1]
            control_ref[t, j : j + 1] = (dot3(x[t], xt[:w]) + xt[w:])[:1]
        dec_ref[j : j + 1] = dec[:1, j * w : (j + 1) * w] / (local * tm)


def shards(tm, dyn_a, dyn_b, gains, defects, state_grad, control_grad, cost_factor, control_factor, init_state):
    local, trajs, w, nu = dyn_b.shape
    high = w + PAD
    knots = local * tm
    rounds = tm.bit_length() - 1
    shape = lambda *s: jax.ShapeDtypeStruct(s, F32)
    vm = pl.BlockSpec(memory_space=pltpu.VMEM)
    elem, end, seg = pl.pallas_call(
        functools.partial(value_kernel, tm),
        out_shape=(shape(local, trajs, high, 2 * w), shape(trajs, high, w), shape(max(local - 1, 1), trajs, high, 2 * w)),
        in_specs=[vm] * 8,
        out_specs=(vm,) * 3,
        scratch_shapes=[
            pltpu.VMEM((max(rounds, 1), trajs, high, 2 * w), F32),
            pltpu.VMEM((max(rounds, 1), trajs, high, 2 * w), F32),
            pltpu.VMEM((high, trajs * w), F32),
            pltpu.VMEM((high, trajs * w), F32),
            pltpu.SemaphoreType.DMA((2, max(rounds, 1))),
        ],
        compiler_params=pltpu.CompilerParams(collective_id=0, has_side_effects=True),
        name="value",
    )(dyn_a, dyn_b, gains, defects, state_grad, control_grad, cost_factor, control_factor)
    new_gains, xt, maps, fold, tot = pl.pallas_call(
        functools.partial(gain_kernel, knots),
        out_shape=(
            shape(local, trajs, nu, w),
            shape(local, trajs, high, nu),
            shape(local, trajs, high, w),
            shape(max(local - 1, 1), trajs, high, w),
            shape(high + 8, trajs * w),
        ),
        in_specs=[vm] * 8,
        out_specs=(vm,) * 5,
        scratch_shapes=[
            pltpu.VMEM((local, trajs, high, w), F32),
            pltpu.VMEM((local * trajs, nu, w + nu + PAD), F32),
        ],
        name="gain",
    )(dyn_a, dyn_b, defects, control_grad, control_factor, elem, seg, end)
    states, controls, feed, dec = pl.pallas_call(
        functools.partial(state_kernel, tm),
        out_shape=(
            shape(local, trajs, w),
            shape(local, trajs, nu),
            shape(local, trajs, nu),
            shape(trajs, w),
        ),
        in_specs=[vm] * 5,
        out_specs=(vm,) * 4,
        scratch_shapes=[
            pltpu.VMEM((max(rounds, 1), high + 8, trajs * w), F32),
            pltpu.VMEM((max(rounds, 1), high + 8, trajs * w), F32),
            pltpu.SemaphoreType.DMA((2, max(rounds, 1))),
        ],
        compiler_params=pltpu.CompilerParams(collective_id=1, has_side_effects=True),
        name="state",
    )(init_state, xt, maps, fold, tot)
    return new_gains, feed, states, controls, dec[:, 0]


def solution(mesh):
    in_specs = (
        P("tm", "grp", None, None),
        P("tm", "grp", None, None),
        P("tm", "grp", None, None),
        P("tm", "grp", None),
        P("tm", "grp", None),
        P("tm", "grp", None),
        P(),
        P(),
        P("grp", None),
    )
    out_specs = (
        P("tm", "grp", None, None),
        P("tm", "grp", None),
        P("tm", "grp", None),
        P("tm", "grp", None),
        P("grp"),
    )
    return jax.shard_map(
        functools.partial(shards, mesh.shape["tm"]),
        mesh=mesh, in_specs=in_specs, out_specs=out_specs, check_vma=False,
    )
```

```python
import functools
import math

import jax
import jax.numpy as jnp
from jax import lax
from jax.experimental import pallas as pl
from jax.experimental.pallas import tpu as pltpu
from jax.sharding import PartitionSpec as P

F32 = jnp.float32
BF16 = jnp.bfloat16
PAD = 8
MESH = pl.DeviceIdType.MESH
NN = (((1,), (0,)), ((), ()))
NT = (((1,), (1,)), ((), ()))


def split(a):
    hi = a.astype(BF16)
    return hi, (a - hi.astype(F32)).astype(BF16)


def dot3(a, b, dims=NN):
    ah, al = split(a)
    bh, bl = split(b)
    left = jnp.concatenate([ah, al, ah], 1)
    right = jnp.concatenate([bh, bh, bl], dims[0][1][0])
    return lax.dot_general(left, right, dimension_numbers=dims, preferred_element_type=F32)


def with_row(matrix, row):
    first = lax.broadcasted_iota(jnp.int32, (PAD, row.shape[1]), 0) == 0
    return jnp.concatenate([matrix, jnp.where(first, row, 0.0)], 0)


def add_tail(a, tail):
    return jnp.concatenate([a[:-PAD], a[-PAD:] + tail], 0)


def compose_value(low, high):
    w = low.shape[1] // 2
    t = add_tail(dot3(low[:, :w], high[:w]), high[w:])
    right = dot3(t[:, w:], low[:w, :w], NT) + low[:, w:]
    return jnp.concatenate([t[:, :w], right], 1)


def apply_value(elem, value):
    w = value.shape[1]
    t = add_tail(dot3(elem[:, :w], value[:w]), value[w:])
    return dot3(t, elem[:w, :w], NT) + elem[:, w:]


def compose_state(low, high):
    w = low.shape[1]
    return add_tail(dot3(low, high[:w]), high[w:])


def place(tm):
    me = lax.axis_index("tm")
    rounds = tm.bit_length() - 1
    bits = [lax.rem(me // (1 << k), 2) for k in range(rounds)]
    partners = [me + (1 << k) * (1 - 2 * bits[k]) for k in range(rounds)]
    return bits, partners


def greet(partners):
    barrier = pltpu.get_barrier_semaphore()
    for partner in partners:
        pl.semaphore_signal(barrier, inc=1, device_id={"tm": partner}, device_id_type=MESH)


def greeted(partners):
    pl.semaphore_wait(pltpu.get_barrier_semaphore(), len(partners))


def exchange(src, dst, sems, k, partner):
    copy = pltpu.make_async_remote_copy(
        src_ref=src,
        dst_ref=dst,
        send_sem=sems.at[0, k],
        recv_sem=sems.at[1, k],
        device_id={"tm": partner},
        device_id_type=MESH,
    )
    copy.start()
    copy.wait()


def value_kernel(
    tm, a_ref, bt_ref, k_ref, d_ref, sg_ref, cg_ref, cf_ref, rf_ref,
    elem_ref, end_ref, seg_ref, send_ref, recv_ref, psend_ref, precv_ref, sems,
):
    local, trajs, nu, w = bt_ref.shape
    knots = local * tm
    scale = 1.0 / math.sqrt(knots)
    bits, partners = place(tm)
    greet(partners)
    eye = lambda n: (
        lax.broadcasted_iota(jnp.int32, (n, n), 0) == lax.broadcasted_iota(jnp.int32, (n, n), 1)
    ).astype(F32)
    term_q = eye(w) + dot3(cf_ref[...], cf_ref[...], NT)
    run_q = term_q / knots
    run_r = eye(nu) + dot3(rf_ref[...], rf_ref[...], NT)
    for t in range(local):
        for j in range(trajs):
            gain = k_ref[t, j]
            gain_t = gain.T
            g_mat = a_ref[t, j].T + dot3(gain_t, bt_ref[t, j])
            left = with_row(dot3(gain_t, run_r), cg_ref[t, j : j + 1])
            right = dot3(left, gain) + with_row(run_q, sg_ref[t, j : j + 1] * scale)
            elem_ref[t, j] = jnp.concatenate(
                [with_row(g_mat, d_ref[t, j : j + 1] * scale), right], 1
            )
    prev, base, count, at = elem_ref, 0, local, 0
    while count > 1:
        for i in range(count // 2):
            for j in range(trajs):
                seg_ref[at + i, j] = compose_value(prev[base + 2 * i, j], prev[base + 2 * i + 1, j])
        prev, base, at, count = seg_ref, at, at + count // 2, count // 2
    greeted(partners)
    totals = [prev[base, j] for j in range(trajs)]
    ident = with_row(
        jnp.concatenate([eye(w), jnp.zeros((w, w), F32)], 1), jnp.zeros((1, 2 * w), F32)
    )
    suffix = [ident] * trajs
    start = with_row(term_q, jnp.zeros((1, w), F32))
    last = len(partners) - 1
    for k in range(last):
        for j in range(trajs):
            send_ref[k, j] = totals[j]
        exchange(send_ref.at[k], recv_ref.at[k], sems, k, partners[k])
        up = bits[k] == 0
        for j in range(trajs):
            other = recv_ref[k, j]
            low = jnp.where(up, totals[j], other)
            high = jnp.where(up, other, totals[j])
            suffix[j] = jnp.where(up, compose_value(suffix[j], other), suffix[j])
            totals[j] = compose_value(low, high)
    if last >= 0:
        psend_ref[...] = jnp.concatenate([apply_value(totals[j], start) for j in range(trajs)], 1)
        exchange(psend_ref, precv_ref, sems, last, partners[last])
        up = bits[last] == 0
        for j in range(trajs):
            came = jnp.where(up, precv_ref[:, j * w : (j + 1) * w], start)
            end_ref[j] = apply_value(suffix[j], came)
    else:
        for j in range(trajs):
            end_ref[j] = start


def gain_kernel(
    knots, a_ref, bt_ref, d_ref, cg_ref, rf_ref, elem_ref, seg_ref, end_ref,
    gain_ref, feed_ref, xt_ref, map_ref, fold_ref, tot_ref, val_ref, aug_ref, sol_ref,
):
    local, trajs, nu, w = bt_ref.shape
    scale = 1.0 / math.sqrt(knots)
    eye = (
        lax.broadcasted_iota(jnp.int32, (nu, nu), 0) == lax.broadcasted_iota(jnp.int32, (nu, nu), 1)
    ).astype(F32)
    run_r = eye + dot3(rf_ref[...], rf_ref[...], NT)
    starts, count, at = [], local // 2, 0
    while count >= 1:
        starts.append(at)
        at += count
        count //= 2
    for j in range(trajs):
        val_ref[local - 1, j] = end_ref[j]
    half = local // 2
    while half >= 1:
        level = half.bit_length() - 1
        for i in range(local // (2 * half)):
            for j in range(trajs):
                hi = 2 * i + 1
                elem = elem_ref[hi, j] if level == 0 else seg_ref[starts[level - 1] + hi, j]
                val_ref[hi * half - 1, j] = apply_value(elem, val_ref[(hi + 1) * half - 1, j])
        half //= 2
    pairs = local * trajs
    lane = lax.broadcasted_iota(jnp.int32, (nu, w + nu + PAD), 1)
    for t in range(local):
        cg_t = cg_ref[t].T
        for j in range(trajs):
            b_t = bt_ref[t, j]
            value = val_ref[t, j]
            rows = with_row(jnp.concatenate([a_ref[t, j].T, b_t], 0), d_ref[t, j : j + 1] * scale)
            y = add_tail(dot3(rows, value[:w]), value[w:])
            aug = dot3(b_t, y, NT)
            aug = aug + jnp.concatenate(
                [jnp.zeros((nu, w), F32), run_r, jnp.zeros((nu, PAD), F32)], 1
            )
            aug = jnp.where(lane == w + nu, aug + cg_t[:, j : j + 1], aug)
            aug_ref[pl.ds(t * trajs + j, nu, stride=pairs)] = jnp.concatenate(
                [aug, jnp.zeros((nu, w - nu - PAD), F32)], 1
            )
    parts = [aug_ref[i * pairs : (i + 1) * pairs] for i in range(nu)]
    for s in range(nu):
        row = parts[s] * (1.0 / parts[s][:, w + s : w + s + 1])
        order = [(s + 1 + i) % nu for i in range(nu - 1)]
        for i in order:
            parts[i] = parts[i] - parts[i][:, w + s : w + s + 1] * row
        parts[s] = row
    for i in range(nu):
        sol_ref[i * pairs : (i + 1) * pairs] = parts[i]
    for t in range(local):
        for j in range(trajs):
            x = sol_ref[pl.ds(t * trajs + j, nu, stride=pairs)]
            gain_ref[t, j] = -x[:, :w]
            x_t = x.T
            xt = -jnp.concatenate([x_t[:w], x_t[w + nu : w + nu + PAD]], 0)
            xt_ref[t, j] = xt
            feed_ref[t, j : j + 1] = xt[w : w + 1]
            map_ref[t, j] = (
                dot3(xt, bt_ref[t, j]) + with_row(a_ref[t, j].T, d_ref[t, j : j + 1] * scale)
            )
    prev, base, count, at = map_ref, 0, local, 0
    while count > 1:
        for i in range(count // 2):
            for j in range(trajs):
                fold_ref[at + i, j] = compose_state(
                    prev[base + 2 * i, j], prev[base + 2 * i + 1, j]
                )
        prev, base, at, count = fold_ref, at, at + count // 2, count // 2
    for j in range(trajs):
        tot_ref[0 : w + PAD, j * w : (j + 1) * w] = prev[base, j]
        total = jnp.zeros((nu, 1), F32)
        for t in range(local):
            aug = aug_ref[pl.ds(t * trajs + j, nu, stride=pairs)]
            feed = xt_ref[t, j][w : w + 1]
            hess_feed = jnp.sum(aug[:, w : w + nu] * feed, 1, keepdims=True)
            back = dot3(eye, xt_ref[t, j][w:], NT)[:, :1]
            total = total + back * (aug[:, w + nu : w + nu + 1] + 0.5 * hess_feed)
        tot_ref[w + PAD :, j * w : (j + 1) * w] = jnp.broadcast_to(
            jnp.sum(total, 0, keepdims=True), (8, w)
        )


def state_kernel(tm, init_ref, tot_ref, start_ref, send_ref, recv_ref, xsend_ref, xrecv_ref, sems):
    trajs, w = init_ref.shape
    high = w + PAD
    bits, partners = place(tm)
    greet(partners)
    row0 = lax.broadcasted_iota(jnp.int32, (PAD, trajs * w), 0) == 0
    eye = (
        lax.broadcasted_iota(jnp.int32, (w, w), 0) == lax.broadcasted_iota(jnp.int32, (w, w), 1)
    ).astype(F32)
    lanes = [slice(j * w, (j + 1) * w) for j in range(trajs)]
    totals = [tot_ref[:high, lanes[j]] for j in range(trajs)]
    dec = tot_ref[high:]
    init = [jnp.broadcast_to(init_ref[j : j + 1], (PAD, w)) for j in range(trajs)]
    before = [with_row(eye, jnp.zeros((1, w), F32))] * trajs
    greeted(partners)
    last = len(partners) - 1
    for k in range(last):
        src = tot_ref
        if k > 0:
            for j in range(trajs):
                send_ref[k, :high, lanes[j]] = totals[j]
            send_ref[k, high:] = dec
            src = send_ref.at[k]
        exchange(src, recv_ref.at[k], sems, k, partners[k])
        dec = dec + recv_ref[k, high:]
        up = bits[k] == 0
        for j in range(trajs):
            other = recv_ref[k, :high, lanes[j]]
            before[j] = jnp.where(up, before[j], compose_state(other, before[j]))
            low = jnp.where(up, totals[j], other)
            top = jnp.where(up, other, totals[j])
            totals[j] = compose_state(low, top)
    if last >= 0:
        ends = [dot3(init[j], totals[j][:w]) + totals[j][w:] for j in range(trajs)]
        xsend_ref[...] = jnp.where(row0, jnp.concatenate(ends, 1), dec)
        exchange(xsend_ref, xrecv_ref, sems, last, partners[last])
        came = xrecv_ref[...]
        dec = dec + came[1:2]
        for j in range(trajs):
            init[j] = jnp.where(
                bits[last] == 0, init[j], jnp.broadcast_to(came[:1, lanes[j]], (PAD, w))
            )
    firsts = [dot3(init[j], before[j][:w]) + before[j][w:] for j in range(trajs)]
    start_ref[...] = jnp.where(row0, jnp.concatenate(firsts, 1), dec)


def rollout_kernel(knots, start_ref, xt_ref, map_ref, fold_ref, state_ref, control_ref, dec_ref):
    local, trajs, high, nu = xt_ref.shape
    w = high - PAD
    starts, count, at = [], local // 2, 0
    while count >= 1:
        starts.append(at)
        at += count
        count //= 2
    for j in range(trajs):
        x = {0: start_ref[:, j * w : (j + 1) * w]}
        half = local // 2
        while half >= 1:
            level = half.bit_length() - 1
            for i in range(local // (2 * half)):
                elem = map_ref[2 * i, j] if level == 0 else fold_ref[starts[level - 1] + 2 * i, j]
                at_t = 2 * i * half
                x[at_t + half] = dot3(x[at_t], elem[:w]) + elem[w:]
            half //= 2
        for t in range(local):
            xt = xt_ref[t, j]
            state_ref[t, j : j + 1] = x[t][:1]
            control_ref[t, j : j + 1] = (dot3(x[t], xt[:w]) + xt[w:])[:1]
        dec_ref[j] = start_ref[1, j * w] / knots


def shards(tm, dyn_a, dyn_b, gains, defects, state_grad, control_grad, cost_factor, control_factor, init_state):
    local, trajs, w, nu = dyn_b.shape
    high = w + PAD
    knots = local * tm
    dyn_bt = jnp.swapaxes(dyn_b, 2, 3)
    rounds = tm.bit_length() - 1
    shape = lambda *s: jax.ShapeDtypeStruct(s, F32)
    vm = pl.BlockSpec(memory_space=pltpu.VMEM)
    elem, end, seg = pl.pallas_call(
        functools.partial(value_kernel, tm),
        out_shape=(shape(local, trajs, high, 2 * w), shape(trajs, high, w), shape(max(local - 1, 1), trajs, high, 2 * w)),
        in_specs=[vm] * 8,
        out_specs=(vm,) * 3,
        scratch_shapes=[
            pltpu.VMEM((max(rounds, 1), trajs, high, 2 * w), F32),
            pltpu.VMEM((max(rounds, 1), trajs, high, 2 * w), F32),
            pltpu.VMEM((high, trajs * w), F32),
            pltpu.VMEM((high, trajs * w), F32),
            pltpu.SemaphoreType.DMA((2, max(rounds, 1))),
        ],
        compiler_params=pltpu.CompilerParams(collective_id=0, has_side_effects=True),
        name="value",
    )(dyn_a, dyn_bt, gains, defects, state_grad, control_grad, cost_factor, control_factor)
    new_gains, feed, xt, maps, fold, tot = pl.pallas_call(
        functools.partial(gain_kernel, knots),
        out_shape=(
            shape(local, trajs, nu, w),
            shape(local, trajs, nu),
            shape(local, trajs, high, nu),
            shape(local, trajs, high, w),
            shape(max(local - 1, 1), trajs, high, w),
            shape(high + 8, trajs * w),
        ),
        in_specs=[vm] * 8,
        out_specs=(vm,) * 6,
        scratch_shapes=[
            pltpu.VMEM((local, trajs, high, w), F32),
            pltpu.VMEM((nu * local * trajs, 2 * w), F32),
            pltpu.VMEM((nu * local * trajs, 2 * w), F32),
        ],
        name="gain",
    )(dyn_a, dyn_bt, defects, control_grad, control_factor, elem, seg, end)
    start = pl.pallas_call(
        functools.partial(state_kernel, tm),
        out_shape=shape(PAD, trajs * w),
        in_specs=[vm] * 2,
        out_specs=vm,
        scratch_shapes=[
            pltpu.VMEM((max(rounds, 1), high + 8, trajs * w), F32),
            pltpu.VMEM((max(rounds, 1), high + 8, trajs * w), F32),
            pltpu.VMEM((PAD, trajs * w), F32),
            pltpu.VMEM((PAD, trajs * w), F32),
            pltpu.SemaphoreType.DMA((2, max(rounds, 1))),
        ],
        compiler_params=pltpu.CompilerParams(collective_id=1, has_side_effects=True),
        name="state",
    )(init_state, tot)
    states, controls, dec = pl.pallas_call(
        functools.partial(rollout_kernel, knots),
        out_shape=(shape(local, trajs, w), shape(local, trajs, nu), shape(trajs)),
        in_specs=[vm] * 4,
        out_specs=(vm, vm, pl.BlockSpec(memory_space=pltpu.SMEM)),
        name="rollout",
    )(start, xt, maps, fold)
    return new_gains, feed, states, controls, dec


def solution(mesh):
    in_specs = (
        P("tm", "grp", None, None),
        P("tm", "grp", None, None),
        P("tm", "grp", None, None),
        P("tm", "grp", None),
        P("tm", "grp", None),
        P("tm", "grp", None),
        P(),
        P(),
        P("grp", None),
    )
    out_specs = (
        P("tm", "grp", None, None),
        P("tm", "grp", None),
        P("tm", "grp", None),
        P("tm", "grp", None),
        P("grp"),
    )
    return jax.shard_map(
        functools.partial(shards, mesh.shape["tm"]),
        mesh=mesh, in_specs=in_specs, out_specs=out_specs, check_vma=False,
    )
```

```python
import functools
import math

import jax
import jax.numpy as jnp
from jax import lax
from jax.experimental import pallas as pl
from jax.experimental.pallas import tpu as pltpu
from jax.sharding import PartitionSpec as P

F32 = jnp.float32
BF16 = jnp.bfloat16
PAD = 8
MESH = pl.DeviceIdType.MESH
NN = (((1,), (0,)), ((), ()))
NT = (((1,), (1,)), ((), ()))


def split(a):
    hi = a.astype(BF16)
    return hi, (a - hi.astype(F32)).astype(BF16)


def dot3(a, b, dims=NN):
    ah, al = split(a)
    bh, bl = split(b)
    left = jnp.concatenate([ah, al, ah], 1)
    right = jnp.concatenate([bh, bh, bl], dims[0][1][0])
    return lax.dot_general(left, right, dimension_numbers=dims, preferred_element_type=F32)


def with_row(matrix, row):
    first = lax.broadcasted_iota(jnp.int32, (PAD, row.shape[1]), 0) == 0
    return jnp.concatenate([matrix, jnp.where(first, row, 0.0)], 0)


def add_tail(a, tail):
    return jnp.concatenate([a[:-PAD], a[-PAD:] + tail], 0)


def compose_value(low, high):
    w = low.shape[1] // 2
    t = add_tail(dot3(low[:, :w], high[:w]), high[w:])
    right = dot3(t[:, w:], low[:w, :w], NT) + low[:, w:]
    return jnp.concatenate([t[:, :w], right], 1)


def apply_value(elem, value):
    w = value.shape[1]
    t = add_tail(dot3(elem[:, :w], value[:w]), value[w:])
    return dot3(t, elem[:w, :w], NT) + elem[:, w:]


def compose_state(low, high):
    w = low.shape[1]
    return add_tail(dot3(low, high[:w]), high[w:])


def place(tm):
    me = lax.axis_index("tm")
    rounds = tm.bit_length() - 1
    bits = [lax.rem(me // (1 << k), 2) for k in range(rounds)]
    partners = [me + (1 << k) * (1 - 2 * bits[k]) for k in range(rounds)]
    return bits, partners


def greet(partners):
    barrier = pltpu.get_barrier_semaphore()
    for partner in partners:
        pl.semaphore_signal(barrier, inc=1, device_id={"tm": partner}, device_id_type=MESH)


def greeted(partners):
    pl.semaphore_wait(pltpu.get_barrier_semaphore(), len(partners))


def send(src, dst, sems, k, partner):
    copy = pltpu.make_async_remote_copy(
        src_ref=src,
        dst_ref=dst,
        send_sem=sems.at[0, k],
        recv_sem=sems.at[1, k],
        device_id={"tm": partner},
        device_id_type=MESH,
    )
    copy.start()
    return copy


def eye_of(n):
    return (
        lax.broadcasted_iota(jnp.int32, (n, n), 0) == lax.broadcasted_iota(jnp.int32, (n, n), 1)
    ).astype(F32)


def fold(leaves, scratch, trajs, compose):
    levels = [leaves]
    at = 0
    while len(levels[-1]) > 1:
        prev = levels[-1]
        level = []
        for i in range(len(prev) // 2):
            (r0, i0), (r1, i1) = prev[2 * i], prev[2 * i + 1]
            for j in range(trajs):
                scratch[at, j] = compose(r0[i0, j], r1[i1, j])
            level.append((scratch, at))
            at += 1
        levels.append(level)
    return levels


def main_kernel(
    tm, a_ref, bt_ref, k_ref, d_ref, sg_ref, cg_ref, cf_ref, rf_ref, init_ref,
    gain_ref, out_ref,
    elem_ref, seg_ref, suf_ref, send_ref, recv_ref, psend_ref, precv_ref,
    rows_ref, const_ref, aug_ref, sol_ref, xt_ref, map_ref, fold_ref, pre_ref,
    ssend_ref, srecv_ref, xsend_ref, xrecv_ref, sems,
):
    local, trajs, nu, w = bt_ref.shape
    high = w + PAD
    knots = local * tm
    pairs = local * trajs
    scale = 1.0 / math.sqrt(knots)
    bits, partners = place(tm)
    greet(partners)
    last = len(partners) - 1
    lanes = [slice(j * w, (j + 1) * w) for j in range(trajs)]
    term_q = eye_of(w) + dot3(cf_ref[...], cf_ref[...], NT)
    run_q = term_q / knots
    run_r = eye_of(nu) + dot3(rf_ref[...], rf_ref[...], NT)
    for t in range(local):
        for j in range(trajs):
            gain = k_ref[t, j]
            gain_t = gain.T
            base = with_row(a_ref[t, j].T, d_ref[t, j : j + 1] * scale)
            rows_ref[t, j, :w] = base[:w]
            rows_ref[t, j, w : w + nu] = bt_ref[t, j]
            rows_ref[t, j, w + nu :] = base[w:]
            g_mat = base[:w] + dot3(gain_t, bt_ref[t, j])
            left = with_row(dot3(gain_t, run_r), cg_ref[t, j : j + 1])
            right = dot3(left, gain) + with_row(run_q, sg_ref[t, j : j + 1] * scale)
            elem_ref[t, j] = jnp.concatenate(
                [jnp.concatenate([g_mat, base[w:]], 0), right], 1
            )
    levels = fold([(elem_ref, t) for t in range(local)], seg_ref, trajs, compose_value)

    def suffixes():
        for t in reversed(range(local - 1)):
            level = ((t + 1) & -(t + 1)).bit_length() - 1
            ref, i = levels[level][(t + 1) >> level]
            end = t + 1 + (1 << level)
            for j in range(trajs):
                whole = ref[i, j]
                suf_ref[t, j] = whole if end == local else compose_value(whole, suf_ref[end - 1, j])

    lane = lax.broadcasted_iota(jnp.int32, (nu, w + nu + PAD), 1)

    def constants(lo, hi):
        for t in range(lo, hi):
            cg_t = cg_ref[t].T
            for j in range(trajs):
                own = jnp.concatenate(
                    [jnp.zeros((nu, w), F32), run_r, jnp.zeros((nu, PAD), F32)], 1
                )
                own = jnp.where(lane == w + nu, own + cg_t[:, j : j + 1], own)
                if t < local - 1:
                    suf = suf_ref[t, j]
                    z = add_tail(dot3(rows_ref[t, j], suf[:w]), suf[w:])
                    rows_ref[t, j] = z[:, :w]
                    own = own + dot3(bt_ref[t, j], z[:, w:], NT)
                const_ref[t, j] = own

    def value_work(k):
        if k == max(last - 2, 0):
            suffixes()
        if k == max(last - 1, 0):
            constants(0, local // 2)
        if k == last:
            constants(local // 2, local)

    greeted(partners)
    ref, i = levels[-1][0]
    totals = [ref[i, j] for j in range(trajs)]
    ident = with_row(
        jnp.concatenate([eye_of(w), jnp.zeros((w, w), F32)], 1), jnp.zeros((1, 2 * w), F32)
    )
    suffix = [ident] * trajs
    start = with_row(term_q, jnp.zeros((1, w), F32))
    for k in range(last):
        for j in range(trajs):
            send_ref[k, j] = totals[j]
        copy = send(send_ref.at[k], recv_ref.at[k], sems, k, partners[k])
        value_work(k)
        copy.wait()
        up = bits[k] == 0
        for j in range(trajs):
            other = recv_ref[k, j]
            suffix[j] = jnp.where(up, compose_value(suffix[j], other), suffix[j])
            totals[j] = compose_value(
                jnp.where(up, totals[j], other), jnp.where(up, other, totals[j])
            )
    psend_ref[...] = jnp.concatenate([apply_value(totals[j], start) for j in range(trajs)], 1)
    copy = send(psend_ref, precv_ref, sems, last, partners[last])
    value_work(last)
    copy.wait()
    up = bits[last] == 0
    ends = [
        apply_value(suffix[j], jnp.where(up, precv_ref[:, lanes[j]], start)) for j in range(trajs)
    ]
    for t in range(local):
        for j in range(trajs):
            rows = rows_ref[t, j]
            y = add_tail(dot3(rows, ends[j][:w]), ends[j][w:])
            aug = dot3(rows[w : w + nu], y, NT) + const_ref[t, j]
            aug_ref[pl.ds(t * trajs + j, nu, stride=pairs)] = jnp.concatenate(
                [aug, jnp.zeros((nu, w - nu - PAD), F32)], 1
            )
    parts = [aug_ref[i * pairs : (i + 1) * pairs] for i in range(nu)]
    for s in range(nu):
        row = parts[s] * (1.0 / parts[s][:, w + s : w + s + 1])
        for i in [(s + 1 + i) % nu for i in range(nu - 1)]:
            parts[i] = parts[i] - parts[i][:, w + s : w + s + 1] * row
        parts[s] = row
    for i in range(nu):
        sol_ref[i * pairs : (i + 1) * pairs] = parts[i]
    for t in range(local):
        for j in range(trajs):
            x = sol_ref[pl.ds(t * trajs + j, nu, stride=pairs)]
            gain_ref[t, j] = -x[:, :w]
            x_t = x.T
            xt = -jnp.concatenate([x_t[:w], x_t[w + nu : w + nu + PAD]], 0)
            xt_ref[t, j] = xt
            map_ref[t, j] = (
                dot3(xt, bt_ref[t, j]) + with_row(a_ref[t, j].T, d_ref[t, j : j + 1] * scale)
            )
    maps = fold([(map_ref, t) for t in range(local)], fold_ref, trajs, compose_state)
    ref, i = maps[-1][0]
    totals = [ref[i, j] for j in range(trajs)]
    decs = []
    for j in range(trajs):
        total = jnp.zeros((nu, 1), F32)
        for t in range(local):
            aug = aug_ref[pl.ds(t * trajs + j, nu, stride=pairs)]
            sol = sol_ref[pl.ds(t * trajs + j, nu, stride=pairs)]
            feed = xt_ref[t, j, w : w + 1]
            hess_feed = jnp.sum(aug[:, w : w + nu] * feed, 1, keepdims=True)
            total = total - sol[:, w + nu : w + nu + 1] * (
                aug[:, w + nu : w + nu + 1] + 0.5 * hess_feed
            )
        decs.append(jnp.broadcast_to(jnp.sum(total, 0, keepdims=True), (PAD, w)))
    dec = jnp.concatenate(decs, 1)

    def prefixes():
        for t in range(local):
            for j in range(trajs):
                xt = xt_ref[t, j]
                if t == 0:
                    pre = with_row(eye_of(w), jnp.zeros((1, w), F32))
                    control = xt
                else:
                    level = (t & -t).bit_length() - 1
                    first = t - (1 << level)
                    ref, i = maps[level][first >> level]
                    pre = ref[i, j]
                    if first > 0:
                        pre = compose_state(pre_ref[first, j, :, :w], pre)
                    control = add_tail(dot3(pre, xt[:w]), xt[w:])
                pre_ref[t, j, :, :w] = pre
                pre_ref[t, j, :, w : w + nu] = control

    row0 = lax.broadcasted_iota(jnp.int32, (PAD, trajs * w), 0) == 0
    init = [jnp.broadcast_to(init_ref[j : j + 1], (PAD, w)) for j in range(trajs)]
    before = [with_row(eye_of(w), jnp.zeros((1, w), F32))] * trajs
    off = last + 1
    for k in range(last):
        for j in range(trajs):
            ssend_ref[k, :high, lanes[j]] = totals[j]
        ssend_ref[k, high:] = dec
        copy = send(ssend_ref.at[k], srecv_ref.at[k], sems, off + k, partners[k])
        if k == max(last - 1, 0):
            prefixes()
        copy.wait()
        dec = dec + srecv_ref[k, high:]
        up = bits[k] == 0
        for j in range(trajs):
            other = srecv_ref[k, :high, lanes[j]]
            before[j] = jnp.where(up, before[j], compose_state(other, before[j]))
            totals[j] = compose_state(
                jnp.where(up, totals[j], other), jnp.where(up, other, totals[j])
            )
    if last == 0:
        prefixes()
    tails = [dot3(init[j], totals[j][:w]) + totals[j][w:] for j in range(trajs)]
    xsend_ref[...] = jnp.where(row0, jnp.concatenate(tails, 1), dec)
    send(xsend_ref, xrecv_ref, sems, off + last, partners[last]).wait()
    came = xrecv_ref[...]
    dec = dec + came[1:2]
    out_ref[pairs:] = dec / knots
    for j in range(trajs):
        first = jnp.where(
            bits[last] == 0, init[j], jnp.broadcast_to(came[:1, lanes[j]], (PAD, w))
        )
        first = dot3(first, before[j][:w]) + before[j][w : w + 1]
        for t in range(local):
            pre = pre_ref[t, j, :, : w + nu]
            both = dot3(first, pre[:w]) + pre[w : w + 1]
            p = t * trajs + j
            out_ref[p : p + 1, : w + nu] = both[:1]
            out_ref[p : p + 1, w + nu : w + 2 * nu] = xt_ref[t, j, w : w + 1]


def unpack_kernel(gain_in, out_in, gain_ref, feed_ref, state_ref, control_ref, dec_ref):
    local, trajs, nu, w = gain_in.shape
    gain_ref[...] = gain_in[...]
    for t in range(local):
        at = slice(t * trajs, (t + 1) * trajs)
        state_ref[t] = out_in[at, :w]
        control_ref[t] = out_in[at, w : w + nu]
        feed_ref[t] = out_in[at, w + nu : w + 2 * nu]
    for j in range(trajs):
        dec_ref[j] = out_in[local * trajs, j * w]


def shards(tm, dyn_a, dyn_b, gains, defects, state_grad, control_grad, cost_factor, control_factor, init_state):
    local, trajs, w, nu = dyn_b.shape
    high = w + PAD
    pairs = local * trajs
    rounds = tm.bit_length() - 1
    shape = lambda *s: jax.ShapeDtypeStruct(s, F32)
    vmem = lambda *s: pltpu.VMEM(s, F32)
    vm = pl.BlockSpec(memory_space=pltpu.VMEM)
    new_gains, out = pl.pallas_call(
        functools.partial(main_kernel, tm),
        out_shape=(shape(local, trajs, nu, w), shape(pairs + PAD, trajs * w)),
        in_specs=[vm] * 9,
        out_specs=(vm, vm),
        scratch_shapes=[
            vmem(local, trajs, high, 2 * w),
            vmem(local, trajs, high, 2 * w),
            vmem(local, trajs, high, 2 * w),
            vmem(rounds, trajs, high, 2 * w),
            vmem(rounds, trajs, high, 2 * w),
            vmem(high, trajs * w),
            vmem(high, trajs * w),
            vmem(local, trajs, w + nu + PAD, w),
            vmem(local, trajs, nu, w + nu + PAD),
            vmem(nu * pairs, 2 * w),
            vmem(nu * pairs, 2 * w),
            vmem(local, trajs, high, nu),
            vmem(local, trajs, high, w),
            vmem(local, trajs, high, w),
            vmem(local, trajs, high, 2 * w),
            vmem(rounds, high + PAD, trajs * w),
            vmem(rounds, high + PAD, trajs * w),
            vmem(PAD, trajs * w),
            vmem(PAD, trajs * w),
            pltpu.SemaphoreType.DMA((2, 2 * rounds)),
        ],
        compiler_params=pltpu.CompilerParams(collective_id=0, has_side_effects=True),
        name="main",
    )(
        dyn_a, jnp.swapaxes(dyn_b, 2, 3), gains, defects, state_grad, control_grad,
        cost_factor, control_factor, init_state,
    )
    new_gains, feed, states, controls, dec = pl.pallas_call(
        unpack_kernel,
        out_shape=(
            shape(local, trajs, nu, w),
            shape(local, trajs, nu),
            shape(local, trajs, w),
            shape(local, trajs, nu),
            shape(trajs),
        ),
        in_specs=[vm] * 2,
        out_specs=(vm,) * 4 + (pl.BlockSpec(memory_space=pltpu.SMEM),),
        name="unpack",
    )(new_gains, out)
    return new_gains, feed, states, controls, dec


def solution(mesh):
    in_specs = (
        P("tm", "grp", None, None),
        P("tm", "grp", None, None),
        P("tm", "grp", None, None),
        P("tm", "grp", None),
        P("tm", "grp", None),
        P("tm", "grp", None),
        P(),
        P(),
        P("grp", None),
    )
    out_specs = (
        P("tm", "grp", None, None),
        P("tm", "grp", None),
        P("tm", "grp", None),
        P("tm", "grp", None),
        P("grp"),
    )
    return jax.shard_map(
        functools.partial(shards, mesh.shape["tm"]),
        mesh=mesh, in_specs=in_specs, out_specs=out_specs, check_vma=False,
    )
```

```python
import functools
import math

import jax
import jax.numpy as jnp
from jax import lax
from jax.experimental import pallas as pl
from jax.experimental.pallas import tpu as pltpu
from jax.sharding import PartitionSpec as P

F32 = jnp.float32
BF16 = jnp.bfloat16
PAD = 8
MESH = pl.DeviceIdType.MESH
NN = (((1,), (0,)), ((), ()))
NT = (((1,), (1,)), ((), ()))


def split(a):
    hi = a.astype(BF16)
    return hi, (a - hi.astype(F32)).astype(BF16)


def stack_left(a):
    hi, lo = split(a)
    return jnp.concatenate([hi, lo, hi], 1)


def stack_right(b, axis=0):
    hi, lo = split(b)
    return jnp.concatenate([hi, hi, lo], axis)


def mul3(left, right, dims=NN):
    return lax.dot_general(left, right, dimension_numbers=dims, preferred_element_type=F32)


def dot3(a, b, dims=NN):
    return mul3(stack_left(a), stack_right(b, dims[0][1][0]), dims)


def with_row(matrix, row):
    first = lax.broadcasted_iota(jnp.int32, (PAD, row.shape[1]), 0) == 0
    return jnp.concatenate([matrix, jnp.where(first, row, 0.0)], 0)


def add_tail(a, tail):
    return jnp.concatenate([a[:-PAD], a[-PAD:] + tail], 0)


def compose_value(low, high):
    w = low.shape[1] // 2
    t = add_tail(dot3(low[:, :w], high[:w]), high[w:])
    right = dot3(t[:, w:], low[:w, :w], NT) + low[:, w:]
    return jnp.concatenate([t[:, :w], right], 1)


def apply_value(elem, value):
    w = value.shape[1]
    t = add_tail(dot3(elem[:, :w], value[:w]), value[w:])
    return dot3(t, elem[:w, :w], NT) + elem[:, w:]


def compose_state(low, high):
    w = low.shape[1]
    return add_tail(dot3(low, high[:w]), high[w:])


def place(tm):
    me = lax.axis_index("tm")
    rounds = tm.bit_length() - 1
    bits = [lax.rem(me // (1 << k), 2) for k in range(rounds)]
    partners = [me + (1 << k) * (1 - 2 * bits[k]) for k in range(rounds)]
    return bits, partners


def greet(partners):
    barrier = pltpu.get_barrier_semaphore()
    for partner in partners:
        pl.semaphore_signal(barrier, inc=1, device_id={"tm": partner}, device_id_type=MESH)


def greeted(partners):
    pl.semaphore_wait(pltpu.get_barrier_semaphore(), len(partners))


def send(src, dst, sems, k, partner):
    copy = pltpu.make_async_remote_copy(
        src_ref=src,
        dst_ref=dst,
        send_sem=sems.at[0, k],
        recv_sem=sems.at[1, k],
        device_id={"tm": partner},
        device_id_type=MESH,
    )
    copy.start()
    return copy


def eye_of(n):
    return (
        lax.broadcasted_iota(jnp.int32, (n, n), 0) == lax.broadcasted_iota(jnp.int32, (n, n), 1)
    ).astype(F32)


def fold(leaves, scratch, trajs, compose):
    levels = [leaves]
    at = 0
    while len(levels[-1]) > 1:
        prev = levels[-1]
        level = []
        for i in range(len(prev) // 2):
            (r0, i0), (r1, i1) = prev[2 * i], prev[2 * i + 1]
            for j in range(trajs):
                scratch[at, j] = compose(r0[i0, j], r1[i1, j])
            level.append((scratch, at))
            at += 1
        levels.append(level)
    return levels


def main_kernel(
    tm, a_ref, bt_ref, k_ref, d_ref, sg_ref, cg_ref, cf_ref, rf_ref, init_ref,
    gain_ref, out_ref,
    elem_ref, seg_ref, suf_ref, send_ref, recv_ref, psend_ref, precv_ref,
    rows_ref, const_ref, aug_ref, sol_ref, xt_ref, map_ref, fold_ref, pre_ref,
    ssend_ref, srecv_ref, xsend_ref, xrecv_ref, base_ref, rows3_ref, pre3_ref, sems,
):
    local, trajs, nu, w = bt_ref.shape
    high = w + PAD
    knots = local * tm
    pairs = local * trajs
    scale = 1.0 / math.sqrt(knots)
    bits, partners = place(tm)
    greet(partners)
    last = len(partners) - 1
    lanes = [slice(j * w, (j + 1) * w) for j in range(trajs)]
    term_q = eye_of(w) + dot3(cf_ref[...], cf_ref[...], NT)
    run_q = term_q / knots
    run_r = eye_of(nu) + dot3(rf_ref[...], rf_ref[...], NT)
    for t in range(local):
        for j in range(trajs):
            gain = k_ref[t, j]
            gain_t = gain.T
            base = with_row(a_ref[t, j].T, d_ref[t, j : j + 1] * scale)
            base_ref[t, j] = base
            rows_ref[t, j, :w] = base[:w]
            rows_ref[t, j, w : w + nu] = bt_ref[t, j]
            rows_ref[t, j, w + nu :] = base[w:]
            g_mat = base[:w] + dot3(gain_t, bt_ref[t, j])
            left = with_row(dot3(gain_t, run_r), cg_ref[t, j : j + 1])
            right = dot3(left, gain) + with_row(run_q, sg_ref[t, j : j + 1] * scale)
            elem_ref[t, j] = jnp.concatenate(
                [jnp.concatenate([g_mat, base[w:]], 0), right], 1
            )
    levels = fold([(elem_ref, t) for t in range(local)], seg_ref, trajs, compose_value)

    def suffixes():
        for t in reversed(range(local - 1)):
            level = ((t + 1) & -(t + 1)).bit_length() - 1
            ref, i = levels[level][(t + 1) >> level]
            end = t + 1 + (1 << level)
            for j in range(trajs):
                whole = ref[i, j]
                suf_ref[t, j] = whole if end == local else compose_value(whole, suf_ref[end - 1, j])

    lane = lax.broadcasted_iota(jnp.int32, (nu, w + nu + PAD), 1)

    def constants(lo, hi):
        for t in range(lo, hi):
            cg_t = cg_ref[t].T
            for j in range(trajs):
                own = jnp.concatenate(
                    [jnp.zeros((nu, w), F32), run_r, jnp.zeros((nu, PAD), F32)], 1
                )
                own = jnp.where(lane == w + nu, own + cg_t[:, j : j + 1], own)
                if t < local - 1:
                    suf = suf_ref[t, j]
                    z = add_tail(dot3(rows_ref[t, j], suf[:w]), suf[w:])
                    rows3_ref[t, j] = stack_left(z[:, :w])
                    own = own + dot3(bt_ref[t, j], z[:, w:], NT)
                else:
                    rows3_ref[t, j] = stack_left(rows_ref[t, j])
                const_ref[t, j] = own

    def value_work(k):
        if k == max(last - 2, 0):
            suffixes()
        if k == max(last - 1, 0):
            constants(0, local // 2)
        if k == last:
            constants(local // 2, local)

    greeted(partners)
    ref, i = levels[-1][0]
    totals = [ref[i, j] for j in range(trajs)]
    ident = with_row(
        jnp.concatenate([eye_of(w), jnp.zeros((w, w), F32)], 1), jnp.zeros((1, 2 * w), F32)
    )
    suffix = [ident] * trajs
    start = with_row(term_q, jnp.zeros((1, w), F32))
    for k in range(last):
        for j in range(trajs):
            send_ref[k, j] = totals[j]
        copy = send(send_ref.at[k], recv_ref.at[k], sems, k, partners[k])
        value_work(k)
        copy.wait()
        up = bits[k] == 0
        for j in range(trajs):
            other = recv_ref[k, j]
            suffix[j] = jnp.where(up, compose_value(suffix[j], other), suffix[j])
            totals[j] = compose_value(
                jnp.where(up, totals[j], other), jnp.where(up, other, totals[j])
            )
    psend_ref[...] = jnp.concatenate([apply_value(totals[j], start) for j in range(trajs)], 1)
    copy = send(psend_ref, precv_ref, sems, last, partners[last])
    value_work(last)
    copy.wait()
    up = bits[last] == 0
    ends = [
        apply_value(suffix[j], jnp.where(up, precv_ref[:, lanes[j]], start)) for j in range(trajs)
    ]
    rights = [stack_right(end[:w]) for end in ends]
    for t in range(local):
        for j in range(trajs):
            rows = rows3_ref[t, j]
            y = add_tail(mul3(rows, rights[j]), ends[j][w:])
            aug = mul3(rows[w : w + nu], stack_right(y, 1), NT) + const_ref[t, j]
            aug_ref[pl.ds(t * trajs + j, nu, stride=pairs)] = jnp.concatenate(
                [aug, jnp.zeros((nu, w - nu - PAD), F32)], 1
            )
    parts = [aug_ref[i * pairs : (i + 1) * pairs] for i in range(nu)]
    for s in range(nu):
        row = parts[s] * (1.0 / parts[s][:, w + s : w + s + 1])
        for i in [(s + 1 + i) % nu for i in range(nu - 1)]:
            parts[i] = parts[i] - parts[i][:, w + s : w + s + 1] * row
        parts[s] = row
    for i in range(nu):
        sol_ref[i * pairs : (i + 1) * pairs] = parts[i]
    for t in range(local):
        for j in range(trajs):
            x = sol_ref[pl.ds(t * trajs + j, nu, stride=pairs)]
            gain_ref[t, j] = -x[:, :w]
            x_t = x.T
            xt = -jnp.concatenate([x_t[:w], x_t[w + nu : w + nu + PAD]], 0)
            xt_ref[t, j] = xt
            map_ref[t, j] = (
                dot3(xt, bt_ref[t, j]) + base_ref[t, j]
            )
    maps = fold([(map_ref, t) for t in range(local)], fold_ref, trajs, compose_state)
    ref, i = maps[-1][0]
    totals = [ref[i, j] for j in range(trajs)]
    decs = []
    for j in range(trajs):
        total = jnp.zeros((nu, 1), F32)
        for t in range(local):
            aug = aug_ref[pl.ds(t * trajs + j, nu, stride=pairs)]
            sol = sol_ref[pl.ds(t * trajs + j, nu, stride=pairs)]
            feed = xt_ref[t, j, w : w + 1]
            hess_feed = jnp.sum(aug[:, w : w + nu] * feed, 1, keepdims=True)
            total = total - sol[:, w + nu : w + nu + 1] * (
                aug[:, w + nu : w + nu + 1] + 0.5 * hess_feed
            )
        decs.append(jnp.broadcast_to(jnp.sum(total, 0, keepdims=True), (PAD, w)))
    dec = jnp.concatenate(decs, 1)

    def prefixes():
        for t in range(local):
            for j in range(trajs):
                xt = xt_ref[t, j]
                if t == 0:
                    pre = with_row(eye_of(w), jnp.zeros((1, w), F32))
                    control = xt
                else:
                    level = (t & -t).bit_length() - 1
                    first = t - (1 << level)
                    ref, i = maps[level][first >> level]
                    pre = ref[i, j]
                    if first > 0:
                        pre = compose_state(pre_ref[first, j, :, :w], pre)
                    control = add_tail(dot3(pre, xt[:w]), xt[w:])
                pre_ref[t, j, :, :w] = pre
                pre_ref[t, j, :, w : w + nu] = control
                pre3_ref[t, j] = stack_right(jnp.concatenate([pre[:w], control[:w]], 1))

    row0 = lax.broadcasted_iota(jnp.int32, (PAD, trajs * w), 0) == 0
    init = [jnp.broadcast_to(init_ref[j : j + 1], (PAD, w)) for j in range(trajs)]
    before = [with_row(eye_of(w), jnp.zeros((1, w), F32))] * trajs
    off = last + 1
    for k in range(last):
        for j in range(trajs):
            ssend_ref[k, :high, lanes[j]] = totals[j]
        ssend_ref[k, high:] = dec
        copy = send(ssend_ref.at[k], srecv_ref.at[k], sems, off + k, partners[k])
        if k == max(last - 1, 0):
            prefixes()
        copy.wait()
        dec = dec + srecv_ref[k, high:]
        up = bits[k] == 0
        for j in range(trajs):
            other = srecv_ref[k, :high, lanes[j]]
            before[j] = jnp.where(up, before[j], compose_state(other, before[j]))
            totals[j] = compose_state(
                jnp.where(up, totals[j], other), jnp.where(up, other, totals[j])
            )
    if last == 0:
        prefixes()
    tails = [dot3(init[j], totals[j][:w]) + totals[j][w:] for j in range(trajs)]
    xsend_ref[...] = jnp.where(row0, jnp.concatenate(tails, 1), dec)
    send(xsend_ref, xrecv_ref, sems, off + last, partners[last]).wait()
    came = xrecv_ref[...]
    dec = dec + came[1:2]
    out_ref[pairs:] = dec / knots
    for j in range(trajs):
        first = jnp.where(
            bits[last] == 0, init[j], jnp.broadcast_to(came[:1, lanes[j]], (PAD, w))
        )
        left = stack_left(dot3(first, before[j][:w]) + before[j][w : w + 1])
        for t in range(local):
            both = mul3(left, pre3_ref[t, j]) + pre_ref[t, j, w : w + 1, : w + nu]
            p = t * trajs + j
            out_ref[p : p + 1, : w + nu] = both[:1]
            out_ref[p : p + 1, w + nu : w + 2 * nu] = xt_ref[t, j, w : w + 1]


def unpack_kernel(gain_in, out_in, gain_ref, feed_ref, state_ref, control_ref, dec_ref):
    local, trajs, nu, w = gain_in.shape
    gain_ref[...] = gain_in[...]
    for t in range(local):
        at = slice(t * trajs, (t + 1) * trajs)
        state_ref[t] = out_in[at, :w]
        control_ref[t] = out_in[at, w : w + nu]
        feed_ref[t] = out_in[at, w + nu : w + 2 * nu]
    for j in range(trajs):
        dec_ref[j] = out_in[local * trajs, j * w]


def shards(tm, dyn_a, dyn_b, gains, defects, state_grad, control_grad, cost_factor, control_factor, init_state):
    local, trajs, w, nu = dyn_b.shape
    high = w + PAD
    pairs = local * trajs
    rounds = tm.bit_length() - 1
    shape = lambda *s: jax.ShapeDtypeStruct(s, F32)
    vmem = lambda *s: pltpu.VMEM(s, F32)
    vm = pl.BlockSpec(memory_space=pltpu.VMEM)
    new_gains, out = pl.pallas_call(
        functools.partial(main_kernel, tm),
        out_shape=(shape(local, trajs, nu, w), shape(pairs + PAD, trajs * w)),
        in_specs=[vm] * 9,
        out_specs=(vm, vm),
        scratch_shapes=[
            vmem(local, trajs, high, 2 * w),
            vmem(local, trajs, high, 2 * w),
            vmem(local, trajs, high, 2 * w),
            vmem(rounds, trajs, high, 2 * w),
            vmem(rounds, trajs, high, 2 * w),
            vmem(high, trajs * w),
            vmem(high, trajs * w),
            vmem(local, trajs, w + nu + PAD, w),
            vmem(local, trajs, nu, w + nu + PAD),
            vmem(nu * pairs, 2 * w),
            vmem(nu * pairs, 2 * w),
            vmem(local, trajs, high, nu),
            vmem(local, trajs, high, w),
            vmem(local, trajs, high, w),
            vmem(local, trajs, high, 2 * w),
            vmem(rounds, high + PAD, trajs * w),
            vmem(rounds, high + PAD, trajs * w),
            vmem(PAD, trajs * w),
            vmem(PAD, trajs * w),
            vmem(local, trajs, high, w),
            pltpu.VMEM((local, trajs, w + nu + PAD, 3 * w), BF16),
            pltpu.VMEM((local, trajs, 3 * w, w + nu), BF16),
            pltpu.SemaphoreType.DMA((2, 2 * rounds)),
        ],
        compiler_params=pltpu.CompilerParams(collective_id=0, has_side_effects=True),
        name="main",
    )(
        dyn_a, jnp.swapaxes(dyn_b, 2, 3), gains, defects, state_grad, control_grad,
        cost_factor, control_factor, init_state,
    )
    new_gains, feed, states, controls, dec = pl.pallas_call(
        unpack_kernel,
        out_shape=(
            shape(local, trajs, nu, w),
            shape(local, trajs, nu),
            shape(local, trajs, w),
            shape(local, trajs, nu),
            shape(trajs),
        ),
        in_specs=[vm] * 2,
        out_specs=(vm,) * 4 + (pl.BlockSpec(memory_space=pltpu.SMEM),),
        name="unpack",
    )(new_gains, out)
    return new_gains, feed, states, controls, dec


def solution(mesh):
    in_specs = (
        P("tm", "grp", None, None),
        P("tm", "grp", None, None),
        P("tm", "grp", None, None),
        P("tm", "grp", None),
        P("tm", "grp", None),
        P("tm", "grp", None),
        P(),
        P(),
        P("grp", None),
    )
    out_specs = (
        P("tm", "grp", None, None),
        P("tm", "grp", None),
        P("tm", "grp", None),
        P("tm", "grp", None),
        P("grp"),
    )
    return jax.shard_map(
        functools.partial(shards, mesh.shape["tm"]),
        mesh=mesh, in_specs=in_specs, out_specs=out_specs, check_vma=False,
    )
```
